256 devices in a mesh: row: 16 (over y, x), col: 16 (over z, core).
Axes of the slice: x: 4, y: 4, z: 8, core: 2. Of those that a mesh axis runs over, the one named last changes fastest.
Arguments:
- matrix: float32 [16384, 16384], P('row', 'col'), may hold values from 0 to 9.5, as said below
Outputs:
- factored: float32 [16384, 16384], P('row', 'col')
The draws below stay inside these ranges and needn't reach their ends.
Inputs may be any that keep to these rules, and one draw needn't show every extreme that they name: `matrix`: symmetric positive definite once the block order is reverted.
All inputs are finite; a program needn't handle non-finite values.
Results may differ from the reference program's by a relative error of at most 0.0003.
Values sent between devices are 32-bit elements; how exact they have to be, the bound alone decides.
A program may use at most 128 MiB of HBM per device.

```python
import jax
import jax.numpy as jnp
from jax import lax

NB = 256
BR = 4
PANELS = 3
BLOCKS = 64
BC = 4
ORDER = 16384


NUGGET = 0.5


SHOWN_RANGE = 0.2


def draw_matrix(key, part):
    place_key = jax.random.fold_in(jax.random.fold_in(key, 7), 0)
    locations = jax.random.uniform(place_key, (ORDER, 2), jnp.float32)
    length_scale = SHOWN_RANGE
    delta_x = locations[:, None, 0] - locations[None, :, 0]
    delta_y = locations[:, None, 1] - locations[None, :, 1]
    distance = jnp.sqrt(delta_x * delta_x + delta_y * delta_y)
    diagonal_ones = (lax.broadcasted_iota(jnp.int32, (ORDER, ORDER), 0) == lax.broadcasted_iota(jnp.int32, (ORDER, ORDER), 1)).astype(jnp.float32)
    covariance = jnp.exp(-distance / length_scale) + NUGGET * diagonal_ones
    grid_rows = BLOCKS // BR
    grid_cols = BLOCKS // BC
    covariance = covariance.reshape(BR, grid_rows, NB, ORDER).transpose(1, 0, 2, 3).reshape(ORDER, ORDER)
    covariance = covariance.reshape(ORDER, BC, grid_cols, NB).transpose(0, 2, 1, 3).reshape(ORDER, ORDER)
    return covariance


def setup_inputs(seed: int = 0) -> dict:
    keys = jax.random.split(jax.random.key(seed), 2)
    return {
        "matrix": draw_matrix(jax.random.fold_in(keys[1], 71), 0),
    }


def reference(matrix):
    grid_rows = BLOCKS // BR
    grid_cols = BLOCKS // BC
    natural = matrix.reshape(grid_rows, BR, NB, grid_cols, BC, NB).transpose(1, 0, 2, 4, 3, 5).reshape(ORDER, ORDER)
    for panel_at in range(PANELS):
        start_at = panel_at * NB
        end_at = start_at + NB
        factor = jnp.linalg.cholesky(natural[start_at:end_at, start_at:end_at])
        solved = jax.scipy.linalg.solve_triangular(factor, natural[end_at:, start_at:end_at].T, lower=True).T
        trailing = natural[end_at:, end_at:] - jnp.dot(solved.astype(jnp.float32), solved.T.astype(jnp.float32), precision=lax.Precision.HIGHEST, preferred_element_type=jnp.float32)
        natural = natural.at[start_at:end_at, start_at:end_at].set(factor)
        natural = natural.at[end_at:, start_at:end_at].set(solved)
        natural = natural.at[end_at:, end_at:].set(trailing)
    block_ids = jnp.arange(ORDER, dtype=jnp.int32) // NB
    zero_mask = (block_ids[:, None] < block_ids[None, :]) & (block_ids[:, None] < PANELS)
    natural = jnp.where(zero_mask, jnp.zeros((), jnp.float32), natural)
    return natural.reshape(BR, grid_rows, NB, BC, grid_cols, NB).transpose(1, 0, 2, 4, 3, 5).reshape(ORDER, ORDER)
```

```python
import functools

import jax
import jax.numpy as jnp
from jax import lax
from jax.experimental import pallas as pl
from jax.experimental.pallas import tpu as pltpu
from jax.sharding import PartitionSpec as P

NB = 256
PANELS = 3
LEAF = 32
MESH = pl.DeviceIdType.MESH
F32 = jnp.float32
BF16 = jnp.bfloat16


def split2(x):
    hi = x.astype(BF16)
    return hi, (x - hi.astype(F32)).astype(BF16)


def split3(x):
    hi = x.astype(BF16)
    rest = x - hi.astype(F32)
    mid = rest.astype(BF16)
    return hi, mid, (rest - mid.astype(F32)).astype(BF16)


def dot_split(a, b, dims):
    d = functools.partial(lax.dot_general, dimension_numbers=(dims, ((), ())), preferred_element_type=F32)
    return d(a[0], b[0]) + (d(a[0], b[1]) + d(a[1], b[0]))


def dot_full(a, b, dims):
    return lax.dot_general(a, b, (dims, ((), ())), precision=lax.Precision.HIGHEST, preferred_element_type=F32)


NN = ((1,), (0,))
NT = ((1,), (1,))
TN = ((0,), (0,))


def factor_panel(work, hooks):
    strips = LEAF // 8
    sub = lax.broadcasted_iota(jnp.int32, (8, 128), 0)
    for leaf in range(NB // LEAF):
        top = leaf * LEAF
        end = top + LEAF
        tiles = [q for q in range(2) if (q + 1) * 128 > top] + [2 + q for q in range(2) if q * 128 < end]
        rows = {
            (t, q): work[top + 8 * t : top + 8 * t + 8, q * 128 : (q + 1) * 128] for t in range(strips) for q in tiles
        }
        for s in range(strips):
            first = top + 8 * s
            q0, at = first // 128, first % 128
            cols = {
                (i, t): jnp.broadcast_to(rows[t, q0][:, at + i : at + i + 1], (8, 128))
                for i in range(8)
                for t in range(s, strips)
            }
            scales = None
            for i in range(8):
                r = lax.rsqrt(jnp.broadcast_to(cols[i, s][i : i + 1, :], (8, 128)))
                scales = r if scales is None else jnp.where(sub == i, r, scales)
                low = {t: cols[i, t] * r for t in range(s, strips)}
                low[s] = jnp.where(sub > i, low[s], 0.0)
                left = range(s + 1 if i == 7 else s, strips)
                for other in range(i + 1, 8):
                    pivot = jnp.broadcast_to(cols[other, s][i : i + 1, :], (8, 128)) * r
                    for t in left:
                        cols[other, t] = cols[other, t] - low[t] * pivot
                for q in tiles:
                    pivot = jnp.broadcast_to(rows[s, q][i : i + 1, :], (8, 128)) * r
                    for t in left:
                        rows[t, q] = rows[t, q] - low[t] * pivot
            for q in tiles:
                work[first : first + 8, q * 128 : (q + 1) * 128] = rows[s, q] * scales
        if end < NB:
            lo, hi = tiles[0] * 128, (tiles[-1] + 1) * 128
            h, m, l = split3(work[top:end, lo:hi])
            rhs = jnp.concatenate([h, m, h, l, m, h], axis=0)
            lhs = jnp.concatenate([v[:, : NB - lo] for v in (h, h, m, h, m, l)], axis=0)
            prod = lax.dot_general(lhs, rhs, (TN, ((), ())), preferred_element_type=F32)
            work[end:, lo:hi] = work[end:, lo:hi] - prod[end - lo :, :]
        if leaf in hooks:
            hooks[leaf]()


def kernel(
    mat, out, held, aj, a11, ai, uj_hi, uj_lo, li_hi, li_lo, urow, work,
    local_sem,
    s_sj, s_si, s_z, s_ax, s_ay, s_j1, s_j2, s_iz, s_ic,
    r_sj, r_si, r_z, r_ax, r_ay, r_j1, r_j2, r_iz, r_ic,
):
    row = lax.axis_index("row")
    col = lax.axis_index("col")
    y, x = row // 4, row % 4
    z, core = col // 2, col % 2

    def copy(src, dst, send, recv, **dev):
        return pltpu.make_async_remote_copy(
            src_ref=src, dst_ref=dst, send_sem=send, recv_sem=recv, device_id=dev, device_id_type=MESH
        )

    barrier = pltpu.get_barrier_semaphore()

    def greet(d, carry):
        pl.semaphore_signal(barrier, inc=1, device_id={"row": (row + d) % 16}, device_id_type=MESH)
        pl.semaphore_signal(barrier, inc=1, device_id={"col": (col + d) % 16}, device_id_type=MESH)
        return carry

    lax.fori_loop(1, 16, greet, 0)
    load = pltpu.make_async_copy(mat, held, local_sem.at[0])
    load.start()
    pl.semaphore_wait(barrier, 30)

    def scatter_j(d):
        p = (row + d) % 16
        return copy(
            mat.at[pl.ds(16 * p, 16), :], aj.at[p // 4, p % 4, row], s_sj.at[d], r_sj.at[row], row=p
        )

    def scatter_i(d):
        p = (col + d) % 16
        return copy(
            mat.at[pl.ds(64 * p, 64), pl.ds(0, NB)], ai.at[p // 2, p % 2, col], s_si.at[d], r_si.at[col], col=p
        )

    def loop(n0, n1, body):
        def step(d, carry):
            body(d)
            return carry

        lax.fori_loop(n0, n1, step, 0)

    @pl.when(row < PANELS)
    def _():
        pltpu.make_async_copy(mat.at[pl.ds(16 * row, 16), :], aj.at[y, x, row], r_sj.at[row]).start()
        loop(1, 16, lambda d: scatter_j(d).start())

    @pl.when(col < PANELS)
    def _():
        pltpu.make_async_copy(
            mat.at[pl.ds(64 * col, 64), pl.ds(0, NB)], ai.at[z, core, col], r_si.at[col]
        ).start()
        loop(1, 16, lambda d: scatter_i(d).start())

    for k in range(PANELS):
        pltpu.make_async_copy(aj.at[y, x, k], aj.at[y, x, k], r_sj.at[k]).wait()

    def spread(k, d):
        return copy(
            aj.at[y, x, k, :, pl.ds(0, NB)],
            a11.at[y, x, k, :, pl.ds(pl.multiple_of(NB * col, NB), NB)],
            s_z.at[k, d], r_z.at[k, col], col=(col + d) % 16,
        )

    for k in range(PANELS):
        @pl.when((col < PANELS) & (col >= k))
        def _():
            pltpu.make_async_copy(
                aj.at[y, x, k, :, pl.ds(0, NB)],
                a11.at[y, x, k, :, pl.ds(pl.multiple_of(NB * col, NB), NB)],
                r_z.at[k, col],
            ).start()
            loop(1, 16, lambda d: spread(k, d).start())

    HALF = 512

    def j_first_x(d):
        return copy(
            aj.at[y, x, :, :, pl.ds(0, HALF)], aj.at[y, x, :, :, pl.ds(0, HALF)],
            s_j1.at[0, d], r_j1.at[0, x], row=y * 4 + (x + d) % 4,
        )

    def j_first_y(d):
        return copy(
            aj.at[y, x, :, :, pl.ds(HALF, HALF)], aj.at[y, x, :, :, pl.ds(HALF, HALF)],
            s_j1.at[1, d], r_j1.at[1, y], row=((y + d) % 4) * 4 + x,
        )

    def j_then_y(d):
        return copy(
            aj.at[y, :, :, :, pl.ds(0, HALF)], aj.at[y, :, :, :, pl.ds(0, HALF)],
            s_j2.at[0, d], r_j2.at[0, y], row=((y + d) % 4) * 4 + x,
        )

    def j_then_x(d):
        return copy(
            aj.at[:, x, :, :, pl.ds(HALF, HALF)], aj.at[:, x, :, :, pl.ds(HALF, HALF)],
            s_j2.at[1, d], r_j2.at[1, x], row=y * 4 + (x + d) % 4,
        )

    def a_x(k, d):
        ref = a11.at[y, x, k, :, pl.ds(NB * k, NB * (PANELS - k))]
        return copy(ref, ref, s_ax.at[k, d], r_ax.at[k, x], row=y * 4 + (x + d) % 4)

    def a_y(k, d):
        ref = a11.at[y, :, k, :, pl.ds(NB * k, NB * (PANELS - k))]
        return copy(ref, ref, s_ay.at[k, d], r_ay.at[k, y], row=((y + d) % 4) * 4 + x)

    def wait_here(ref, sem):
        pltpu.make_async_copy(ref, ref, sem).wait()

    for k in range(PANELS):
        for j in range(k, PANELS):
            wait_here(a11.at[y, x, k, :, pl.ds(NB * j, NB)], r_z.at[k, j])
        loop(1, 4, lambda d: a_x(k, d).start())
    for k in range(PANELS):
        for d in range(1, 4):
            src = (x + d) % 4
            wait_here(a11.at[y, src, k, :, pl.ds(NB * k, NB * (PANELS - k))], r_ax.at[k, src])
        loop(1, 4, lambda d: a_y(k, d).start())
        if k == 0:
            loop(1, 4, lambda d: j_first_x(d).start())
            loop(1, 4, lambda d: j_first_y(d).start())

    def i_ring(d):
        return copy(
            ai.at[z, core], ai.at[z, core], s_iz.at[d], r_iz.at[z], col=((z + d) % 8) * 2 + core
        )

    def i_core(src):
        return copy(
            ai.at[src, core], ai.at[src, core], s_ic.at[src], r_ic.at[src], col=z * 2 + 1 - core
        )

    for k in range(PANELS):
        wait_here(ai.at[z, core, k], r_si.at[k])
    loop(1, 8, lambda d: i_ring(d).start())
    i_core(z).start()

    def wait_a11(k):
        for d in range(1, 4):
            src = (y + d) % 4
            wait_here(a11.at[src, :, k, :, pl.ds(NB * k, NB * (PANELS - k))], r_ay.at[k, src])

    def forward_j():
        for d in range(1, 4):
            src = (x + d) % 4
            wait_here(aj.at[y, src, :, :, pl.ds(0, HALF)], r_j1.at[0, src])
        loop(1, 4, lambda d: j_then_y(d).start())
        for d in range(1, 4):
            src = (y + d) % 4
            wait_here(aj.at[src, x, :, :, pl.ds(HALF, HALF)], r_j1.at[1, src])
        loop(1, 4, lambda d: j_then_x(d).start())

    def forward_i():
        def step(d):
            src = (z + d) % 8
            wait_here(ai.at[src, core], r_iz.at[src])
            i_core(src).start()

        loop(1, 8, step)

    def finish_bulk():
        for d in range(1, 4):
            src = (y + d) % 4
            wait_here(aj.at[src, :, :, :, pl.ds(0, HALF)], r_j2.at[0, src])
        for d in range(1, 4):
            src = (x + d) % 4
            wait_here(aj.at[:, src, :, :, pl.ds(HALF, HALF)], r_j2.at[1, src])
        loop(0, 8, lambda src: wait_here(ai.at[src, 1 - core], r_ic.at[src]))

    eye = (
        lax.broadcasted_iota(jnp.int32, (NB, NB), 0) == lax.broadcasted_iota(jnp.int32, (NB, NB), 1)
    ).astype(F32)
    for k in range(PANELS):
        wait_a11(k)
        lo = NB * k
        diag = a11[:, :, k, :, lo : lo + NB].reshape(NB, NB)
        for kk in range(k):
            u = urow[kk, :, lo - NB : lo]
            diag = diag - dot_full(u, u, TN)
        work[:, :NB] = diag
        work[:, NB:] = eye
        factor_panel(work, {0: forward_j, 4: forward_i} if k == 0 else {})
        inv = work[:, NB:]
        inv2 = split2(inv)
        if k < PANELS - 1:
            rest = a11[:, :, k, :, lo + NB :].reshape(NB, -1)
            for kk in range(k):
                rest = rest - dot_full(urow[kk, :, lo - NB : lo], urow[kk, :, lo:], TN)
            urow[k, :, lo : 2 * NB] = dot_full(inv, rest, NN)
        if k == 0:
            finish_bulk()
        for ch in range(4):
            at = slice(NB * ch, NB * ch + NB)
            rhs = aj[:, :, k, :, at].reshape(NB, NB)
            lhs = ai[2 * ch : 2 * ch + 2, :, k].reshape(NB, NB)
            for kk in range(k):
                u2 = split2(urow[kk, :, lo - NB : lo])
                rhs = rhs - dot_split(u2, (uj_hi[kk, :, at], uj_lo[kk, :, at]), TN)
                lhs = lhs - dot_split((li_hi[kk, at], li_lo[kk, at]), u2, NN)
            hi, low = split2(dot_split(inv2, split2(rhs), NN))
            uj_hi[k, :, at] = hi
            uj_lo[k, :, at] = low
            full = dot_split(split2(lhs), inv2, NT)
            hi, low = split2(full)
            li_hi[k, at] = hi
            li_lo[k, at] = low

    load.wait()

    for ch in range(4):
        at = slice(NB * ch, NB * ch + NB)
        for cc in range(4):
            to = slice(NB * cc, NB * cc + NB)
            total = held[at, to]
            for k in range(PANELS):
                total = total - dot_split((li_hi[k, at], li_lo[k, at]), (uj_hi[k, :, to], uj_lo[k, :, to]), NN)
            held[at, to] = total

    @pl.when(row < PANELS)
    def _():
        held[:NB, :] = jnp.zeros((NB, 4 * NB), F32)

    rr = lax.broadcasted_iota(jnp.int32, (NB, NB), 0)
    cc = lax.broadcasted_iota(jnp.int32, (NB, NB), 1)
    for k in range(PANELS):
        @pl.when(col == k)
        def _():
            first = li_hi[k, :NB].astype(F32) + li_lo[k, :NB].astype(F32)
            keep = (row > k) | ((row == k) & (rr >= cc))
            held[:NB, :NB] = jnp.where(keep, first, 0.0)
            held[NB:, :NB] = li_hi[k, NB:].astype(F32) + li_lo[k, NB:].astype(F32)

    store = pltpu.make_async_copy(held, out, local_sem.at[1])
    store.start()

    @pl.when(row < PANELS)
    def _():
        loop(1, 16, lambda d: scatter_j(d).wait_send())

    @pl.when(col < PANELS)
    def _():
        loop(1, 16, lambda d: scatter_i(d).wait_send())

    for k in range(PANELS):
        @pl.when((col < PANELS) & (col >= k))
        def _():
            loop(1, 16, lambda d: spread(k, d).wait_send())

        loop(1, 4, lambda d: a_x(k, d).wait_send())
        loop(1, 4, lambda d: a_y(k, d).wait_send())
    for c in (j_first_x, j_first_y, j_then_y, j_then_x):
        loop(1, 4, lambda d: c(d).wait_send())
    loop(1, 8, lambda d: i_ring(d).wait_send())
    loop(0, 8, lambda d: i_core(d).wait_send())
    store.wait()


def body(matrix):
    rows = matrix.shape[0]
    dma = pltpu.SemaphoreType.DMA
    groups = [(16,), (16,), (3, 16), (3, 4), (3, 4), (2, 4), (2, 4), (8,), (8,)]
    landed = [(3,), (3,), (3, 3), (3, 4), (3, 4), (2, 4), (2, 4), (8,), (8,)]
    return pl.pallas_call(
        kernel,
        out_shape=jax.ShapeDtypeStruct(matrix.shape, F32),
        in_specs=[pl.BlockSpec(memory_space=pl.ANY)],
        out_specs=pl.BlockSpec(memory_space=pl.ANY),
        scratch_shapes=[
            pltpu.VMEM(matrix.shape, F32),
            pltpu.VMEM((4, 4, PANELS, 16, rows), F32),
            pltpu.VMEM((4, 4, PANELS, 16, PANELS * NB), F32),
            pltpu.VMEM((8, 2, PANELS, 64, NB), F32),
            pltpu.VMEM((PANELS, NB, rows), BF16),
            pltpu.VMEM((PANELS, NB, rows), BF16),
            pltpu.VMEM((PANELS, rows, NB), BF16),
            pltpu.VMEM((PANELS, rows, NB), BF16),
            pltpu.VMEM((PANELS - 1, NB, (PANELS - 1) * NB), F32),
            pltpu.VMEM((NB, 2 * NB), F32),
            dma((2,)),
        ]
        + [dma(g) for g in groups]
        + [dma(g) for g in landed],
        compiler_params=pltpu.CompilerParams(
            collective_id=0, has_side_effects=True, vmem_limit_bytes=56 * 1024 * 1024
        ),
    )(matrix)


def solution(mesh):
    return jax.shard_map(body, mesh=mesh, in_specs=(P("row", "col"),), out_specs=P("row", "col"), check_vma=False)
```

```python
import functools

import jax
import jax.numpy as jnp
from jax import lax
from jax.experimental import pallas as pl
from jax.experimental.pallas import tpu as pltpu
from jax.sharding import PartitionSpec as P

NB = 256
PANELS = 3
LEAF = 32
MESH = pl.DeviceIdType.MESH
F32 = jnp.float32
BF16 = jnp.bfloat16


LEFT = (0, 0, 1, 0, 1, 2)
RIGHT = (0, 1, 0, 2, 1, 0)


def split3(x):
    hi = x.astype(BF16)
    rest = x - hi.astype(F32)
    mid = rest.astype(BF16)
    return hi, mid, (rest - mid.astype(F32)).astype(BF16)


def dot_parts(a, b, dims):
    lhs = jnp.concatenate([a[i] for i in LEFT], axis=dims[0][0])
    rhs = jnp.concatenate([b[i] for i in RIGHT], axis=dims[1][0])
    return lax.dot_general(lhs, rhs, (dims, ((), ())), preferred_element_type=F32)


NN = ((1,), (0,))
NT = ((1,), (1,))
TN = ((0,), (0,))
FIRST = (0, 1, 3)


def factor_panel(work, hooks):
    strips = LEAF // 8
    sub = lax.broadcasted_iota(jnp.int32, (8, 128), 0)
    for leaf in range(NB // LEAF):
        top = leaf * LEAF
        end = top + LEAF
        tiles = [q for q in range(2) if (q + 1) * 128 > top] + [2 + q for q in range(2) if q * 128 < end]
        rows = {
            (t, q): work[top + 8 * t : top + 8 * t + 8, q * 128 : (q + 1) * 128] for t in range(strips) for q in tiles
        }
        for s in range(strips):
            first = top + 8 * s
            q0, at = first // 128, first % 128
            cols = {
                (i, t): jnp.broadcast_to(rows[t, q0][:, at + i : at + i + 1], (8, 128))
                for i in range(8)
                for t in range(s, strips)
            }
            scales = None
            for i in range(8):
                r = lax.rsqrt(jnp.broadcast_to(cols[i, s][i : i + 1, :], (8, 128)))
                scales = r if scales is None else jnp.where(sub == i, r, scales)
                low = {t: cols[i, t] * r for t in range(s, strips)}
                low[s] = jnp.where(sub > i, low[s], 0.0)
                left = range(s + 1 if i == 7 else s, strips)
                for other in range(i + 1, 8):
                    pivot = jnp.broadcast_to(cols[other, s][i : i + 1, :], (8, 128)) * r
                    for t in left:
                        cols[other, t] = cols[other, t] - low[t] * pivot
                for q in tiles:
                    pivot = jnp.broadcast_to(rows[s, q][i : i + 1, :], (8, 128)) * r
                    for t in left:
                        rows[t, q] = rows[t, q] - low[t] * pivot
            for q in tiles:
                work[first : first + 8, q * 128 : (q + 1) * 128] = rows[s, q] * scales
        if end < NB:
            lo, hi = tiles[0] * 128, (tiles[-1] + 1) * 128
            h, m, l = split3(work[top:end, lo:hi])
            rhs = jnp.concatenate([h, m, h, l, m, h], axis=0)
            lhs = jnp.concatenate([v[:, : NB - lo] for v in (h, h, m, h, m, l)], axis=0)
            prod = lax.dot_general(lhs, rhs, (TN, ((), ())), preferred_element_type=F32)
            work[end:, lo:hi] = work[end:, lo:hi] - prod[end - lo :, :]
        if leaf in hooks:
            hooks[leaf]()


def kernel(
    mat, out, held, aj, lead, ai, uj, li, urow, winv, work,
    local_sem,
    s_sa, s_sj, s_si, s_z, s_al, s_ac, s_j1, s_j2, s_j3, s_iz, s_ic,
    r_sa, r_sj, r_si, r_z, r_al, r_ac, r_j1, r_j2, r_j3, r_iz, r_ic,
):
    row = lax.axis_index("row")
    col = lax.axis_index("col")
    y, x = row // 4, row % 4
    z, core = col // 2, col % 2
    owner = (row == 0) & (col == 0)

    def copy(src, dst, send, recv, **dev):
        return pltpu.make_async_remote_copy(
            src_ref=src, dst_ref=dst, send_sem=send, recv_sem=recv, device_id=dev, device_id_type=MESH
        )

    def wait_here(ref, sem):
        pltpu.make_async_copy(ref, ref, sem).wait()

    def loop(n0, n1, body):
        def step(d, carry):
            body(d)
            return carry

        lax.fori_loop(n0, n1, step, 0)

    def row_at(dy, dx):
        return ((y + dy) % 4) * 4 + (x + dx) % 4

    def col_at(dz):
        return ((z + dz) % 8) * 2 + core

    barrier = pltpu.get_barrier_semaphore()

    def greet(**dev):
        pl.semaphore_signal(barrier, inc=1, device_id=dev, device_id_type=MESH)

    for k in range(PANELS):
        @pl.when(col != k)
        def _():
            greet(col=k)

    loop(1, 16, lambda d: greet(row=(row + d) % 16))
    for d in (1, 2, 6, 7):
        greet(col=col_at(d))
    greet(col=z * 2 + 1 - core)

    load = pltpu.make_async_copy(mat, held, local_sem.at[0])

    lead_at = col * (col + 1) // 2 + row

    def scatter_a(d):
        p = (row + d) % 16
        return copy(
            mat.at[pl.ds(16 * p, 16), pl.ds(0, NB)], lead.at[lead_at, p],
            s_sa.at[d], r_sa.at[row], row=p,
        )

    def scatter_w(p):
        return copy(work.at[pl.ds(16 * p, 16), pl.ds(NB, NB)], lead.at[0, p], s_sa.at[p], r_sa.at[0], row=p)

    def scatter_j(d):
        p = (row + d) % 16
        return copy(mat.at[pl.ds(16 * p, 16), :], aj.at[row, p // 4, p % 4], s_sj.at[d], r_sj.at[row], row=p)

    def scatter_i(d):
        p = (col + d) % 16
        return copy(
            mat.at[pl.ds(64 * p, 64), pl.ds(0, NB)], ai.at[col, p // 2, p % 2], s_si.at[d], r_si.at[col], col=p
        )

    has_lead = (row < PANELS) & (col < PANELS) & (row <= col) & (col > 0)

    def enter():
        pl.semaphore_wait(
            barrier, 20 + 15 * (col < PANELS).astype(jnp.int32)
        )

        @pl.when(has_lead)
        def _():
            pltpu.make_async_copy(
                mat.at[pl.ds(16 * row, 16), pl.ds(0, NB)], lead.at[lead_at, row], r_sa.at[row]
            ).start()
            loop(1, 16, lambda d: scatter_a(d).start())

        @pl.when(col < PANELS)
        def _():
            pltpu.make_async_copy(
                mat.at[pl.ds(64 * col, 64), pl.ds(0, NB)], ai.at[col, z, core], r_si.at[col]
            ).start()
            loop(1, 16, lambda d: scatter_i(d).start())

        @pl.when(row < PANELS)
        def _():
            pltpu.make_async_copy(mat.at[pl.ds(16 * row, 16), :], aj.at[row, y, x], r_sj.at[row]).start()
            loop(1, 16, lambda d: scatter_j(d).start())

    eye = (
        lax.broadcasted_iota(jnp.int32, (NB, NB), 0) == lax.broadcasted_iota(jnp.int32, (NB, NB), 1)
    ).astype(F32)

    @pl.when(owner)
    def _():
        first = pltpu.make_async_copy(mat.at[pl.ds(0, NB), pl.ds(0, NB)], work.at[:, pl.ds(0, NB)], local_sem.at[1])
        first.start()
        first.wait()
        work[:, NB:] = eye
        factor_panel(
            work,
            {
                3: lambda: (enter(), loop(1, 8, lambda p: scatter_w(p).start())),
                4: lambda: loop(8, 10, lambda p: scatter_w(p).start()),
                5: lambda: loop(10, 12, lambda p: scatter_w(p).start()),
                6: lambda: loop(12, 14, lambda p: scatter_w(p).start()),
            },
        )
        loop(14, 16, lambda p: scatter_w(p).start())
        lead[0, 0] = work[:16, NB:]
        load.start()

    @pl.when(jnp.logical_not(owner))
    def _():
        enter()
        load.start()

    def spread(j, d):
        ref = lead.at[pl.ds(FIRST[j], j + 1), row]
        return copy(ref, ref, s_z.at[d], r_z.at[j], col=(col + d) % 16 if j == 0 else col_at(d))

    def relay(j):
        @pl.when(col == j)
        def _():
            if j == 0:
                @pl.when(row > 0)
                def _():
                    wait_here(lead.at[0, row], r_sa.at[0])
            else:
                for k in range(j + 1):
                    wait_here(lead.at[FIRST[j] + k, row], r_sa.at[k])
            loop(1, 8 if j else 16, lambda d: spread(j, d).start())

    def lead_all(j, d):
        ref = lead.at[pl.ds(FIRST[j], j + 1), row]
        return copy(ref, ref, s_al.at[j, d], r_al.at[j, row], row=(row + d) % 16)

    def lead_core(j):
        ref = lead.at[pl.ds(FIRST[j], j + 1)]
        return copy(ref, ref, s_ac.at[j], r_ac.at[j], col=z * 2 + 1 - core)

    def carries(j):
        return core == j % 2 if j else core >= 0

    def send_lead(j):
        @pl.when(carries(j))
        def _():
            @pl.when(col != j)
            def _():
                wait_here(lead.at[pl.ds(FIRST[j], j + 1), row], r_z.at[j])

            loop(1, 16, lambda d: lead_all(j, d).start())

    def gather_lead(j):
        @pl.when(carries(j))
        def _():
            def arrive(d):
                src = (row + d) % 16
                wait_here(lead.at[pl.ds(FIRST[j], j + 1), src], r_al.at[j, src])

            loop(1, 16, arrive)
            if j:
                lead_core(j).start()

    def wait_lead(j):
        @pl.when(core != j % 2)
        def _():
            wait_here(lead.at[pl.ds(FIRST[j], j + 1)], r_ac.at[j])

    HALF = 512
    LOW, HIGH = pl.ds(0, HALF), pl.ds(HALF, HALF)

    def j_first(k, h, d):
        ref = aj.at[k, y, x, :, (LOW, HIGH)[h]]
        if h == 0:
            return copy(ref, ref, s_j1.at[k, h, d], r_j1.at[k, h, x], row=row_at(0, d))
        return copy(ref, ref, s_j1.at[k, h, d], r_j1.at[k, h, y], row=row_at(d, 0))

    def j_group(k, h, at, part):
        inner = (slice(None), pl.ds(0, 2), pl.ds(2, 2))[part]
        if h == 0:
            return aj.at[k, at, inner, :, LOW]
        return aj.at[k, inner, at, :, HIGH]

    def j_dev(h, d):
        return row_at(d, 0) if h == 0 else row_at(0, d)

    def j_mine(h):
        return y if h == 0 else x

    def j_second(k, h, way):
        ref = j_group(k, h, j_mine(h), 0)
        return copy(ref, ref, s_j2.at[k, h, way], r_j2.at[k, h, way], row=j_dev(h, (1, 3)[way]))

    def j_third(k, h, way):
        ref = j_group(k, h, (j_mine(h) + (3, 1)[way]) % 4, 1 + way)
        return copy(ref, ref, s_j3.at[k, h, way], r_j3.at[k, h, way], row=j_dev(h, (1, 3)[way]))

    def bulk_j1(k):
        wait_here(aj.at[k, y, x], r_sj.at[k])
        for h in range(2):
            loop(1, 4, lambda d: j_first(k, h, d).start())

    def bulk_j2(k):
        for h in range(2):
            for d in range(1, 4):
                src = (j_mine(1 - h) + d) % 4
                ref = aj.at[k, y, src, :, LOW] if h == 0 else aj.at[k, src, x, :, HIGH]
                wait_here(ref, r_j1.at[k, h, src])
            for way in range(2):
                j_second(k, h, way).start()

    def bulk_j3(k):
        for h in range(2):
            for way in range(2):
                wait_here(j_group(k, h, (j_mine(h) + (3, 1)[way]) % 4, 0), r_j2.at[k, h, way])
                j_third(k, h, way).start()

    def bulk_j4(k):
        for h in range(2):
            for way in range(2):
                wait_here(j_group(k, h, (j_mine(h) + 2) % 4, 1 + way), r_j3.at[k, h, way])

    STEPS = ((1, 0), (2, 0), (7, 0), (6, 0), (1, 6), (2, 6), (7, 2), (6, 2))

    def i_piece(k, n, at):
        if n == 5:
            return ai.at[k, at, core, pl.ds(0, 32)]
        if n == 7:
            return ai.at[k, at, core, pl.ds(32, 32)]
        return ai.at[k, at, core]

    def i_ring(k, n):
        far, whose = STEPS[n]
        ref = i_piece(k, n, (z + whose) % 8)
        return copy(ref, ref, s_iz.at[k, n], r_iz.at[k, n], col=col_at(far))

    def i_arrive(k, n):
        far, whose = STEPS[n]
        wait_here(i_piece(k, n, (z + whose + 8 - far) % 8), r_iz.at[k, n])

    def i_core(k, at):
        ref = ai.at[k, at % 8, core]
        return copy(ref, ref, s_ic.at[k, at % 8], r_ic.at[k, at % 8], col=z * 2 + 1 - core)

    def bulk_i(k, step):
        if step == 0:
            wait_here(ai.at[k, z, core], r_si.at[k])
            for n in range(4):
                i_ring(k, n).start()
            i_core(k, z).start()
        elif step == 1:
            for n in (1, 3):
                i_arrive(k, n)
            for n in range(4, 8):
                i_ring(k, n).start()
            for n in (0, 2):
                i_arrive(k, n)
            for at in (1, 2, 6, 7):
                i_core(k, z + at).start()
        else:
            for n in range(4, 8):
                i_arrive(k, n)
            for at in (3, 4, 5):
                i_core(k, z + at).start()

    def bulk_i_end(k):
        loop(0, 8, lambda at: wait_here(ai.at[k, at, 1 - core], r_ic.at[k, at]))

    def each(f, *args):
        for k in range(PANELS):
            f(k, *args)

    relay(1)
    relay(2)
    relay(0)
    send_lead(1)
    send_lead(2)
    each(bulk_i, 0)
    send_lead(0)
    gather_lead(1)
    each(bulk_j1)
    gather_lead(0)

    hooks = [
        {},
        {
            0: lambda: each(bulk_i, 1),
            2: lambda: gather_lead(2),
            4: lambda: each(bulk_j2),
        },
        {
            0: lambda: each(bulk_i, 2),
            2: lambda: each(bulk_j3),
        },
    ]

    @pl.when(owner)
    def _():
        loop(1, 16, lambda p: scatter_w(p).wait_send())

    def block(kk, j):
        return split3(urow[kk, :, NB * (j - 1) : NB * j])

    for k in range(PANELS):
        if k == 0:
            wait_lead(1)
            winv[0] = lead[0].reshape(NB, NB)
        else:
            if k == 2:
                wait_lead(2)
                urow[0, :, NB:] = dot_parts(split3(winv[0]), split3(lead[3].reshape(NB, NB)), NN)
                t = lead[4].reshape(NB, NB) - dot_parts(block(0, 1), block(0, 2), TN)
                urow[1, :, NB:] = dot_parts(split3(winv[1]), split3(t), NN)
            diag = lead[FIRST[k] + k].reshape(NB, NB)
            for kk in range(k):
                u = block(kk, k)
                diag = diag - dot_parts(u, u, TN)
            work[:, :NB] = diag
            work[:, NB:] = eye
            factor_panel(work, hooks[k])
            winv[k] = work[:, NB:]
        if k == 0:
            urow[0, :, :NB] = dot_parts(split3(winv[0]), split3(lead[1].reshape(NB, NB)), NN)

    for k in range(PANELS):
        bulk_j4(k)
        bulk_i_end(k)
        inv = split3(winv[k])
        for ch in range(4):
            at = slice(NB * ch, NB * ch + NB)
            rhs = aj[k, :, :, :, at].reshape(NB, NB)
            lhs = ai[k, 2 * ch : 2 * ch + 2].reshape(NB, NB)
            for kk in range(k):
                u = block(kk, k)
                rhs = rhs - dot_parts(u, [uj[kk, i, :, at] for i in range(3)], TN)
                lhs = lhs - dot_parts([li[kk, i, at] for i in range(3)], u, NN)
            for i, part in enumerate(split3(dot_parts(inv, split3(rhs), NN))):
                uj[k, i, :, at] = part
            for i, part in enumerate(split3(dot_parts(split3(lhs), inv, NT))):
                li[k, i, at] = part

    load.wait()

    for ch in range(4):
        at = slice(NB * ch, NB * ch + NB)
        for cc in range(4):
            to = slice(NB * cc, NB * cc + NB)
            lhs = jnp.concatenate([li[k, i, at] for k in range(PANELS) for i in LEFT], axis=1)
            rhs = jnp.concatenate([uj[k, i, :, to] for k in range(PANELS) for i in RIGHT], axis=0)
            held[at, to] = held[at, to] - jnp.dot(lhs, rhs, preferred_element_type=F32)

    @pl.when(row < PANELS)
    def _():
        held[:NB, :] = jnp.zeros((NB, 4 * NB), F32)

    rr = lax.broadcasted_iota(jnp.int32, (NB, NB), 0)
    cc = lax.broadcasted_iota(jnp.int32, (NB, NB), 1)

    def joined(k, at):
        return li[k, 0, at].astype(F32) + (li[k, 1, at].astype(F32) + li[k, 2, at].astype(F32))

    for k in range(PANELS):
        @pl.when(col == k)
        def _():
            keep = (row > k) | ((row == k) & (rr >= cc))
            held[:NB, :NB] = jnp.where(keep, joined(k, slice(0, NB)), 0.0)
            held[NB:, :NB] = joined(k, slice(NB, 4 * NB))

    store = pltpu.make_async_copy(held, out, local_sem.at[1])
    store.start()

    @pl.when(has_lead)
    def _():
        loop(1, 16, lambda d: scatter_a(d).wait_send())

    @pl.when(row < PANELS)
    def _():
        loop(1, 16, lambda d: scatter_j(d).wait_send())

    @pl.when(col < PANELS)
    def _():
        loop(1, 16, lambda d: scatter_i(d).wait_send())

    for j in range(PANELS):
        @pl.when(col == j)
        def _():
            loop(1, 8 if j else 16, lambda d: spread(j, d).wait_send())

        @pl.when(carries(j))
        def _():
            loop(1, 16, lambda d: lead_all(j, d).wait_send())
            if j:
                lead_core(j).wait_send()

    for k in range(PANELS):
        for h in range(2):
            loop(1, 4, lambda d: j_first(k, h, d).wait_send())
            for way in range(2):
                j_second(k, h, way).wait_send()
                j_third(k, h, way).wait_send()
        for n in range(8):
            i_ring(k, n).wait_send()
        loop(0, 8, lambda at: i_core(k, at).wait_send())
    store.wait()


def body(matrix):
    rows = matrix.shape[0]
    dma = pltpu.SemaphoreType.DMA
    sent = [(16,), (16,), (16,), (16,), (3, 16), (3,), (3, 2, 4), (3, 2, 2), (3, 2, 2), (3, 8), (3, 8)]
    landed = [(3,), (3,), (3,), (3,), (3, 16), (3,), (3, 2, 4), (3, 2, 2), (3, 2, 2), (3, 8), (3, 8)]
    return pl.pallas_call(
        kernel,
        out_shape=jax.ShapeDtypeStruct(matrix.shape, F32),
        in_specs=[pl.BlockSpec(memory_space=pl.ANY)],
        out_specs=pl.BlockSpec(memory_space=pl.ANY),
        scratch_shapes=[
            pltpu.VMEM(matrix.shape, F32),
            pltpu.VMEM((PANELS, 4, 4, 16, rows), F32),
            pltpu.VMEM((6, 16, 16, NB), F32),
            pltpu.VMEM((PANELS, 8, 2, 64, NB), F32),
            pltpu.VMEM((PANELS, 3, NB, rows), BF16),
            pltpu.VMEM((PANELS, 3, rows, NB), BF16),
            pltpu.VMEM((PANELS - 1, NB, (PANELS - 1) * NB), F32),
            pltpu.VMEM((PANELS, NB, NB), F32),
            pltpu.VMEM((NB, 2 * NB), F32),
            dma((2,)),
        ]
        + [dma(g) for g in sent]
        + [dma(g) for g in landed],
        compiler_params=pltpu.CompilerParams(
            collective_id=0, has_side_effects=True, vmem_limit_bytes=56 * 1024 * 1024
        ),
    )(matrix)


def solution(mesh):
    return jax.shard_map(body, mesh=mesh, in_specs=(P("row", "col"),), out_specs=P("row", "col"), check_vma=False)
```

```python
import functools

import jax
import jax.numpy as jnp
from jax import lax
from jax.experimental import pallas as pl
from jax.experimental.pallas import tpu as pltpu
from jax.sharding import PartitionSpec as P

NB = 256
PANELS = 3
LEAF = 32
MESH = pl.DeviceIdType.MESH
F32 = jnp.float32
BF16 = jnp.bfloat16


LEFT = (0, 0, 1, 0, 1, 2)
RIGHT = (0, 1, 0, 2, 1, 0)


def split3(x):
    hi = x.astype(BF16)
    rest = x - hi.astype(F32)
    mid = rest.astype(BF16)
    return hi, mid, (rest - mid.astype(F32)).astype(BF16)


def dot_parts(a, b, dims):
    lhs = jnp.concatenate([a[i] for i in LEFT], axis=dims[0][0])
    rhs = jnp.concatenate([b[i] for i in RIGHT], axis=dims[1][0])
    return lax.dot_general(lhs, rhs, (dims, ((), ())), preferred_element_type=F32)


NN = ((1,), (0,))
NT = ((1,), (1,))
TN = ((0,), (0,))
FIRST = (0, 1, 3)


def factor_panel(work, hooks):
    strips = LEAF // 8
    sub = lax.broadcasted_iota(jnp.int32, (8, 128), 0)
    for leaf in range(NB // LEAF):
        top = leaf * LEAF
        end = top + LEAF
        tiles = [q for q in range(2) if (q + 1) * 128 > top] + [2 + q for q in range(2) if q * 128 < end]
        rows = {
            (t, q): work[top + 8 * t : top + 8 * t + 8, q * 128 : (q + 1) * 128] for t in range(strips) for q in tiles
        }
        for s in range(strips):
            first = top + 8 * s
            q0, at = first // 128, first % 128
            cols = {
                (i, t): jnp.broadcast_to(rows[t, q0][:, at + i : at + i + 1], (8, 128))
                for i in range(8)
                for t in range(s, strips)
            }
            scales = None
            for i in range(8):
                r = lax.rsqrt(jnp.broadcast_to(cols[i, s][i : i + 1, :], (8, 128)))
                scales = r if scales is None else jnp.where(sub == i, r, scales)
                low = {t: cols[i, t] * r for t in range(s, strips)}
                low[s] = jnp.where(sub > i, low[s], 0.0)
                left = range(s + 1 if i == 7 else s, strips)
                for other in range(i + 1, 8):
                    pivot = jnp.broadcast_to(cols[other, s][i : i + 1, :], (8, 128)) * r
                    for t in left:
                        cols[other, t] = cols[other, t] - low[t] * pivot
                for q in tiles:
                    pivot = jnp.broadcast_to(rows[s, q][i : i + 1, :], (8, 128)) * r
                    for t in left:
                        rows[t, q] = rows[t, q] - low[t] * pivot
            for q in tiles:
                work[first : first + 8, q * 128 : (q + 1) * 128] = rows[s, q] * scales
        if end < NB:
            lo, hi = tiles[0] * 128, (tiles[-1] + 1) * 128
            h, m, l = split3(work[top:end, lo:hi])
            rhs = jnp.concatenate([h, m, h, l, m, h], axis=0)
            lhs = jnp.concatenate([v[:, : NB - lo] for v in (h, h, m, h, m, l)], axis=0)
            prod = lax.dot_general(lhs, rhs, (TN, ((), ())), preferred_element_type=F32)
            work[end:, lo:hi] = work[end:, lo:hi] - prod[end - lo :, :]
        if leaf in hooks:
            hooks[leaf]()


def kernel(
    mat, out, held, aj, lead, ai, uj, li, urow, winv, work,
    local_sem,
    s_sa, s_sj, s_si, s_z, s_al, s_ac, s_j1, s_j2, s_j3, s_iz, s_ic,
    r_sa, r_sj, r_si, r_z, r_al, r_ac, r_j1, r_j2, r_j3, r_iz, r_ic,
):
    row = lax.axis_index("row")
    col = lax.axis_index("col")
    y, x = row // 4, row % 4
    z, core = col // 2, col % 2
    owner = (row == 0) & (col == 0)

    def copy(src, dst, send, recv, **dev):
        return pltpu.make_async_remote_copy(
            src_ref=src, dst_ref=dst, send_sem=send, recv_sem=recv, device_id=dev, device_id_type=MESH
        )

    def wait_here(ref, sem):
        pltpu.make_async_copy(ref, ref, sem).wait()

    def loop(n0, n1, body):
        def step(d, carry):
            body(d)
            return carry

        lax.fori_loop(n0, n1, step, 0)

    def row_at(dy, dx):
        return ((y + dy) % 4) * 4 + (x + dx) % 4

    def col_at(dz):
        return ((z + dz) % 8) * 2 + core

    barrier = pltpu.get_barrier_semaphore()

    def greet(**dev):
        pl.semaphore_signal(barrier, inc=1, device_id=dev, device_id_type=MESH)

    for k in range(PANELS):
        @pl.when(col != k)
        def _():
            greet(col=k)

    loop(1, 16, lambda d: greet(row=(row + d) % 16))
    for d in (1, 2, 6, 7):
        greet(col=col_at(d))
    greet(col=z * 2 + 1 - core)

    load = pltpu.make_async_copy(mat, held, local_sem.at[0])

    lead_at = col * (col + 1) // 2 + row

    def scatter_a(d):
        p = (row + d) % 16
        return copy(
            mat.at[pl.ds(16 * p, 16), pl.ds(0, NB)], lead.at[lead_at, p],
            s_sa.at[d], r_sa.at[row], row=p,
        )

    def scatter_w(p):
        return copy(work.at[pl.ds(16 * p, 16), pl.ds(NB, NB)], lead.at[0, p], s_sa.at[p], r_sa.at[0], row=p)

    def scatter_j(d):
        p = (row + d) % 16
        return copy(mat.at[pl.ds(16 * p, 16), :], aj.at[row, p // 4, p % 4], s_sj.at[d], r_sj.at[row], row=p)

    def scatter_i(d):
        p = (col + d) % 16
        return copy(
            mat.at[pl.ds(64 * p, 64), pl.ds(0, NB)], ai.at[col, p // 2, p % 2], s_si.at[d], r_si.at[col], col=p
        )

    has_lead = (row < PANELS) & (col < PANELS) & (row <= col) & (col > 0)

    def enter():
        pl.semaphore_wait(
            barrier, 20 + 15 * (col < PANELS).astype(jnp.int32)
        )

        @pl.when(has_lead)
        def _():
            pltpu.make_async_copy(
                mat.at[pl.ds(16 * row, 16), pl.ds(0, NB)], lead.at[lead_at, row], r_sa.at[row]
            ).start()
            loop(1, 16, lambda d: scatter_a(d).start())

        @pl.when(col < PANELS)
        def _():
            pltpu.make_async_copy(
                mat.at[pl.ds(64 * col, 64), pl.ds(0, NB)], ai.at[col, z, core], r_si.at[col]
            ).start()
            loop(1, 16, lambda d: scatter_i(d).start())

        @pl.when(row < PANELS)
        def _():
            pltpu.make_async_copy(mat.at[pl.ds(16 * row, 16), :], aj.at[row, y, x], r_sj.at[row]).start()
            loop(1, 16, lambda d: scatter_j(d).start())

    eye = (
        lax.broadcasted_iota(jnp.int32, (NB, NB), 0) == lax.broadcasted_iota(jnp.int32, (NB, NB), 1)
    ).astype(F32)

    @pl.when(owner)
    def _():
        first = pltpu.make_async_copy(mat.at[pl.ds(0, NB), pl.ds(0, NB)], work.at[:, pl.ds(0, NB)], local_sem.at[1])
        first.start()
        first.wait()
        work[:, NB:] = eye
        factor_panel(
            work,
            {
                3: lambda: (enter(), loop(1, 8, lambda p: scatter_w(p).start())),
                4: lambda: loop(8, 10, lambda p: scatter_w(p).start()),
                5: lambda: loop(10, 12, lambda p: scatter_w(p).start()),
                6: lambda: loop(12, 14, lambda p: scatter_w(p).start()),
            },
        )
        loop(14, 16, lambda p: scatter_w(p).start())
        lead[0, 0] = work[:16, NB:]
        load.start()

    @pl.when(jnp.logical_not(owner))
    def _():
        enter()
        load.start()

    def spread(j, d):
        ref = lead.at[pl.ds(FIRST[j], j + 1), row]
        return copy(ref, ref, s_z.at[d], r_z.at[j], col=(col + d) % 16 if j == 0 else col_at(d))

    def relay(j):
        @pl.when(col == j)
        def _():
            if j == 0:
                @pl.when(row > 0)
                def _():
                    wait_here(lead.at[0, row], r_sa.at[0])
            else:
                for k in range(j + 1):
                    wait_here(lead.at[FIRST[j] + k, row], r_sa.at[k])
            loop(1, 8 if j else 16, lambda d: spread(j, d).start())

    def lead_all(j, d):
        ref = lead.at[pl.ds(FIRST[j], j + 1), row]
        return copy(ref, ref, s_al.at[j, d], r_al.at[j, row], row=(row + d) % 16)

    def lead_core(j):
        ref = lead.at[pl.ds(FIRST[j], j + 1)]
        return copy(ref, ref, s_ac.at[j], r_ac.at[j], col=z * 2 + 1 - core)

    def carries(j):
        return core == j % 2 if j else core >= 0

    def send_lead(j):
        @pl.when(carries(j))
        def _():
            @pl.when(col != j)
            def _():
                wait_here(lead.at[pl.ds(FIRST[j], j + 1), row], r_z.at[j])

            loop(1, 16, lambda d: lead_all(j, d).start())

    def gather_lead(j):
        @pl.when(carries(j))
        def _():
            def arrive(d):
                src = (row + d) % 16
                wait_here(lead.at[pl.ds(FIRST[j], j + 1), src], r_al.at[j, src])

            loop(1, 16, arrive)
            if j:
                lead_core(j).start()

    def wait_lead(j):
        @pl.when(core != j % 2)
        def _():
            wait_here(lead.at[pl.ds(FIRST[j], j + 1)], r_ac.at[j])

    HALF = 512
    LOW, HIGH = pl.ds(0, HALF), pl.ds(HALF, HALF)

    def j_first(k, h, d):
        ref = aj.at[k, y, x, :, (LOW, HIGH)[h]]
        if h == 0:
            return copy(ref, ref, s_j1.at[k, h, d], r_j1.at[k, h, x], row=row_at(0, d))
        return copy(ref, ref, s_j1.at[k, h, d], r_j1.at[k, h, y], row=row_at(d, 0))

    def j_group(k, h, at, part):
        inner = (slice(None), pl.ds(0, 2), pl.ds(2, 2))[part]
        if h == 0:
            return aj.at[k, at, inner, :, LOW]
        return aj.at[k, inner, at, :, HIGH]

    def j_dev(h, d):
        return row_at(d, 0) if h == 0 else row_at(0, d)

    def j_mine(h):
        return y if h == 0 else x

    def j_second(k, h, way):
        ref = j_group(k, h, j_mine(h), 0)
        return copy(ref, ref, s_j2.at[k, h, way], r_j2.at[k, h, way], row=j_dev(h, (1, 3)[way]))

    def j_third(k, h, way):
        ref = j_group(k, h, (j_mine(h) + (3, 1)[way]) % 4, 1 + way)
        return copy(ref, ref, s_j3.at[k, h, way], r_j3.at[k, h, way], row=j_dev(h, (1, 3)[way]))

    def bulk_j1(k):
        wait_here(aj.at[k, y, x], r_sj.at[k])
        for h in range(2):
            loop(1, 4, lambda d: j_first(k, h, d).start())

    def bulk_j2(k):
        for h in range(2):
            for d in range(1, 4):
                src = (j_mine(1 - h) + d) % 4
                ref = aj.at[k, y, src, :, LOW] if h == 0 else aj.at[k, src, x, :, HIGH]
                wait_here(ref, r_j1.at[k, h, src])
            for way in range(2):
                j_second(k, h, way).start()

    def bulk_j3(k):
        for h in range(2):
            for way in range(2):
                wait_here(j_group(k, h, (j_mine(h) + (3, 1)[way]) % 4, 0), r_j2.at[k, h, way])
                j_third(k, h, way).start()

    def bulk_j4(k):
        for h in range(2):
            for way in range(2):
                wait_here(j_group(k, h, (j_mine(h) + 2) % 4, 1 + way), r_j3.at[k, h, way])

    STEPS = ((1, 0), (2, 0), (7, 0), (6, 0), (1, 6), (2, 6), (7, 2), (6, 2))

    def i_piece(k, n, at):
        if n == 5:
            return ai.at[k, at, core, pl.ds(0, 32)]
        if n == 7:
            return ai.at[k, at, core, pl.ds(32, 32)]
        return ai.at[k, at, core]

    def i_ring(k, n):
        far, whose = STEPS[n]
        ref = i_piece(k, n, (z + whose) % 8)
        return copy(ref, ref, s_iz.at[k, n], r_iz.at[k, n], col=col_at(far))

    def i_arrive(k, n):
        far, whose = STEPS[n]
        wait_here(i_piece(k, n, (z + whose + 8 - far) % 8), r_iz.at[k, n])

    def i_core(k, at):
        ref = ai.at[k, at % 8, core]
        return copy(ref, ref, s_ic.at[k, at % 8], r_ic.at[k, at % 8], col=z * 2 + 1 - core)

    def bulk_i(k, step):
        if step == 0:
            wait_here(ai.at[k, z, core], r_si.at[k])
            for n in range(4):
                i_ring(k, n).start()
            i_core(k, z).start()
        elif step == 1:
            for n in (1, 3):
                i_arrive(k, n)
            for n in range(4, 8):
                i_ring(k, n).start()
            for n in (0, 2):
                i_arrive(k, n)
            for at in (1, 2, 6, 7):
                i_core(k, z + at).start()
        else:
            for n in range(4, 8):
                i_arrive(k, n)
            for at in (3, 4, 5):
                i_core(k, z + at).start()

    def bulk_i_end(k):
        loop(0, 8, lambda at: wait_here(ai.at[k, at, 1 - core], r_ic.at[k, at]))

    def each(f, *args):
        for k in range(PANELS):
            f(k, *args)

    relay(1)
    relay(2)
    relay(0)
    send_lead(1)
    send_lead(2)
    each(bulk_i, 0)
    send_lead(0)
    gather_lead(1)
    each(bulk_j1)
    gather_lead(0)

    hooks = [
        {},
        {
            0: lambda: each(bulk_i, 1),
            2: lambda: gather_lead(2),
            4: lambda: each(bulk_j2),
        },
        {
            0: lambda: each(bulk_i, 2),
            2: lambda: each(bulk_j3),
        },
    ]

    @pl.when(owner)
    def _():
        loop(1, 16, lambda p: scatter_w(p).wait_send())

    def block(kk, j):
        return split3(urow[kk, :, NB * (j - 1) : NB * j])

    for k in range(PANELS):
        if k == 0:
            wait_lead(1)
            winv[0] = lead[0].reshape(NB, NB)
        else:
            if k == 2:
                wait_lead(2)
                urow[0, :, NB:] = dot_parts(split3(winv[0]), split3(lead[3].reshape(NB, NB)), NN)
                t = lead[4].reshape(NB, NB) - dot_parts(block(0, 1), block(0, 2), TN)
                urow[1, :, NB:] = dot_parts(split3(winv[1]), split3(t), NN)
            diag = lead[FIRST[k] + k].reshape(NB, NB)
            for kk in range(k):
                u = block(kk, k)
                diag = diag - dot_parts(u, u, TN)
            work[:, :NB] = diag
            work[:, NB:] = eye
            factor_panel(work, hooks[k])
            winv[k] = work[:, NB:]
        if k == 0:
            urow[0, :, :NB] = dot_parts(split3(winv[0]), split3(lead[1].reshape(NB, NB)), NN)

    for k in range(PANELS):
        bulk_j4(k)
        bulk_i_end(k)
        inv = split3(winv[k])
        for ch in range(4):
            at = slice(NB * ch, NB * ch + NB)
            rhs = aj[k, :, :, :, at].reshape(NB, NB)
            lhs = ai[k, 2 * ch : 2 * ch + 2].reshape(NB, NB)
            for kk in range(k):
                u = block(kk, k)
                rhs = rhs - dot_parts(u, [uj[kk, i, :, at] for i in range(3)], TN)
                lhs = lhs - dot_parts([li[kk, i, at] for i in range(3)], u, NN)
            for i, part in enumerate(split3(dot_parts(inv, split3(rhs), NN))):
                uj[k, i, :, at] = part
            for i, part in enumerate(split3(dot_parts(split3(lhs), inv, NT))):
                li[k, i, at] = part

    load.wait()

    rr = lax.broadcasted_iota(jnp.int32, (NB, NB), 0)
    cols_at = lax.broadcasted_iota(jnp.int32, (NB, NB), 1)

    def store(ch):
        band = pl.ds(NB * ch, NB)
        return pltpu.make_async_copy(held.at[band], out.at[band], local_sem.at[2 + ch])

    for ch in range(4):
        at = slice(NB * ch, NB * ch + NB)
        for cc in range(4):
            to = slice(NB * cc, NB * cc + NB)
            lhs = jnp.concatenate([li[k, i, at] for k in range(PANELS) for i in LEFT], axis=1)
            rhs = jnp.concatenate([uj[k, i, :, to] for k in range(PANELS) for i in RIGHT], axis=0)
            held[at, to] = held[at, to] - jnp.dot(lhs, rhs, preferred_element_type=F32)
        if ch == 0:
            @pl.when(row < PANELS)
            def _():
                held[:NB, :] = jnp.zeros((NB, 4 * NB), F32)

        for k in range(PANELS):
            @pl.when(col == k)
            def _():
                value = li[k, 0, at].astype(F32) + (li[k, 1, at].astype(F32) + li[k, 2, at].astype(F32))
                if ch == 0:
                    value = jnp.where((row > k) | ((row == k) & (rr >= cols_at)), value, 0.0)
                held[at, :NB] = value

        store(ch).start()

    @pl.when(has_lead)
    def _():
        loop(1, 16, lambda d: scatter_a(d).wait_send())

    @pl.when(row < PANELS)
    def _():
        loop(1, 16, lambda d: scatter_j(d).wait_send())

    @pl.when(col < PANELS)
    def _():
        loop(1, 16, lambda d: scatter_i(d).wait_send())

    for j in range(PANELS):
        @pl.when(col == j)
        def _():
            loop(1, 8 if j else 16, lambda d: spread(j, d).wait_send())

        @pl.when(carries(j))
        def _():
            loop(1, 16, lambda d: lead_all(j, d).wait_send())
            if j:
                lead_core(j).wait_send()

    for k in range(PANELS):
        for h in range(2):
            loop(1, 4, lambda d: j_first(k, h, d).wait_send())
            for way in range(2):
                j_second(k, h, way).wait_send()
                j_third(k, h, way).wait_send()
        for n in range(8):
            i_ring(k, n).wait_send()
        loop(0, 8, lambda at: i_core(k, at).wait_send())
    for ch in range(4):
        store(ch).wait()


def body(matrix):
    rows = matrix.shape[0]
    dma = pltpu.SemaphoreType.DMA
    sent = [(16,), (16,), (16,), (16,), (3, 16), (3,), (3, 2, 4), (3, 2, 2), (3, 2, 2), (3, 8), (3, 8)]
    landed = [(3,), (3,), (3,), (3,), (3, 16), (3,), (3, 2, 4), (3, 2, 2), (3, 2, 2), (3, 8), (3, 8)]
    return pl.pallas_call(
        kernel,
        out_shape=jax.ShapeDtypeStruct(matrix.shape, F32),
        in_specs=[pl.BlockSpec(memory_space=pl.ANY)],
        out_specs=pl.BlockSpec(memory_space=pl.ANY),
        scratch_shapes=[
            pltpu.VMEM(matrix.shape, F32),
            pltpu.VMEM((PANELS, 4, 4, 16, rows), F32),
            pltpu.VMEM((6, 16, 16, NB), F32),
            pltpu.VMEM((PANELS, 8, 2, 64, NB), F32),
            pltpu.VMEM((PANELS, 3, NB, rows), BF16),
            pltpu.VMEM((PANELS, 3, rows, NB), BF16),
            pltpu.VMEM((PANELS - 1, NB, (PANELS - 1) * NB), F32),
            pltpu.VMEM((PANELS, NB, NB), F32),
            pltpu.VMEM((NB, 2 * NB), F32),
            dma((6,)),
        ]
        + [dma(g) for g in sent]
        + [dma(g) for g in landed],
        compiler_params=pltpu.CompilerParams(
            collective_id=0, has_side_effects=True, vmem_limit_bytes=56 * 1024 * 1024
        ),
    )(matrix)


def solution(mesh):
    return jax.shard_map(body, mesh=mesh, in_specs=(P("row", "col"),), out_specs=P("row", "col"), check_vma=False)
```
